32 devices in a mesh: dp: 8 (over z, core), expert: 4 (over y, x).
Axes of the slice: x: 2, y: 2, z: 4, core: 2. Of those that a mesh axis runs over, the one named last changes fastest.
Arguments:
- tokens: bfloat16 [1024, 2048], P('dp', 'expert'), may hold values from -6 to 6
- routes: int32 [1024, 4], P('dp'), may hold values from 0 to 7, all different within a row; in each aligned block of 128 rows (0 to 127, 128 to 255, ...) at most 80 rows name the same one
- gate_weights: float32 [1024, 4], P('dp'), may hold values from 0.1 to 1
- gate_up_weight: bfloat16 [8, 2048, 2, 2816], P('dp', None, None, 'expert'), may hold values from -0.125 to 0.125
- down_weight: bfloat16 [8, 2816, 2048], P('dp', 'expert'), may hold values from -0.109375 to 0.109375
Outputs:
- combined: bfloat16 [1024, 2048], P('dp', 'expert')
The draws below stay inside these ranges and needn't reach their ends.
Inputs may be any that keep to these rules, and one draw needn't show every extreme that they name: `routes`: each row names 4 different experts. Within the 128 rows of one dp shard no expert is named more than 80 times, and in every draw some expert is named exactly 80 times within some shard.
All inputs are finite; a program needn't handle non-finite values.
Results may differ from the reference program's by a relative error of at most 0.015.
Values may be sent and summed in bfloat16 or wider, within the bound.
No kernel may reach another device: no remote copies, remote signals or barrier semaphores. Data moves between devices by JAX's collectives and lax.ppermute only.
A program may use at most 64 MiB of HBM per device.

```python
import math
import jax
import jax.numpy as jnp
import numpy as np
from jax import lax

D = 2048
FF = 2816
TOPK = 4
TOK_DEV = 128
EXPERTS = 8
CAP = 80
TOKENS = 1024
N_DP = 8
N_EXPERT = 4


def block_levels(stream_key, dims, cuts, least, high):
    def one(axis_at, blocks):
        steps = jax.random.uniform(jax.random.fold_in(jax.random.fold_in(stream_key, 6), axis_at), (blocks,), jnp.float32, least / len(cuts), high / len(cuts))
        return jnp.repeat(jnp.exp(steps), dims[axis_at] // blocks).reshape((-1,) + (1,) * (len(dims) - axis_at - 1))

    factor_of = one(*cuts[0])
    for cut in cuts[1:]:
        factor_of = factor_of * one(*cut)
    return factor_of


def deal_out(own_key, own, number, rows, amount, top, bound, slope):
    sequence = jax.random.permutation(own_key, amount)
    crowded, ordinary = portions_of(amount, rows * top, bound, slope, True), portions_of(amount, rows * top, bound, slope, False)
    places = jnp.arange(amount)

    def named(tallies, rotation):
        used = int((tallies > 0).sum())
        fixed = max(1, used // 4)
        shifted = fixed + (places - fixed + rotation * (used - fixed)) % max(1, amount - fixed)
        return jnp.zeros((amount,), jnp.int32).at[sequence[jnp.where(places < fixed, places, shifted)]].set(jnp.asarray(tallies, jnp.int32))

    tallies = jnp.where(number % 4 == 0, named(crowded, number // 4), named(ordinary, number - number // 4 - 1))
    mixed = jax.random.permutation(jax.random.fold_in(own, 3), amount)
    source_of, sink = mixed[0:amount // 2 * 2:2], mixed[1:amount // 2 * 2:2]
    room = jnp.minimum(tallies[source_of] - 1, bound - tallies[sink]) // 2
    room = jnp.where((source_of == sequence[0]) | (sink == sequence[0]) | (tallies[sink] == 0), 0, jnp.maximum(room, 0))
    shifted = jax.random.randint(jax.random.fold_in(own, 4), (amount // 2,), 0, 1 << 20) % (room + 1)
    tallies = tallies.at[source_of].add(-shifted).at[sink].add(shifted)
    labels = jnp.searchsorted(jnp.cumsum(tallies), jnp.arange(rows * top), side="right").astype(jnp.int32)
    grid = labels.reshape(top, rows).T
    grid = grid[jax.random.permutation(jax.random.fold_in(own, 1), rows)]
    rotation = jax.random.randint(jax.random.fold_in(own, 2), (rows, 1), 0, top)
    return jnp.take_along_axis(grid, (jnp.arange(top)[None, :] + rotation) % top, axis=1)


def portions_of(number_of, total, reach, skew, full):
    loads = [(1 << 20) // math.isqrt(grade ** skew) + 1 for grade in range(1, number_of + 1)]
    largest = reach if full else min(reach, max(-(-total // number_of), total * loads[0] // sum(loads)))
    least = 1 if total - largest >= number_of - 1 else 0
    holding, surplus = [largest] + [least] * (number_of - 1), total - largest - least * (number_of - 1)
    while surplus > 0:
        candidates = [i for i in range(1, number_of) if holding[i] < largest] or [i for i in range(1, number_of) if holding[i] < reach]
        pool, remaining = sum([loads[i] for i in candidates]), surplus
        for i in candidates:
            addition = min(reach - holding[i], max(1, remaining * loads[i] // pool), surplus)
            holding[i] = holding[i] + addition
            surplus = surplus - addition
    return np.array(holding)


def noise(rng, shape, deviation, most, cuts=(), kind=jnp.bfloat16):
    gain = block_levels(rng, shape, cuts, -0.22, 0.18) if cuts else 1.0
    values = jax.random.normal(rng, shape, jnp.float32) * deviation * gain
    return jnp.minimum(jnp.maximum(values, -most), most).astype(kind)


def setup_inputs(seed: int = 0) -> dict:
    streams_of = jax.random.split(jax.random.key(seed), 6)
    tokens = noise(streams_of[0], (TOKENS, D), 1.0, 6.0, ((0, 8), (1, 4)))
    routes_keys = jax.random.split(jax.random.fold_in(streams_of[1], 1), TOKENS // TOK_DEV)
    routes_turns = jax.random.permutation(jax.random.fold_in(streams_of[1], 3), TOKENS // TOK_DEV)
    routes = jax.vmap(lambda own, number: deal_out(jax.random.fold_in(streams_of[1], 2), own, number, TOK_DEV, EXPERTS, TOPK, CAP, 2))(routes_keys, routes_turns).reshape((TOKENS, TOPK))
    gate_weights = jnp.clip(jnp.exp(math.log(1.0) - 2.3025851 * jax.random.uniform(streams_of[2], (TOKENS, TOPK), jnp.float32) ** block_levels(streams_of[2], (TOKENS, TOPK), ((0, 8),), -0.2, 0.2)), 0.1, 1.0)
    gate_up_weight = noise(streams_of[3], (EXPERTS, D, 2, FF), D ** -0.5, 0.125, ((0, 8), (3, 4)))
    down_weight = noise(streams_of[4], (EXPERTS, FF, D), FF ** -0.5, 0.109375, ((0, 8), (1, 4)))
    return dict(tokens=tokens, routes=routes, gate_weights=gate_weights, gate_up_weight=gate_up_weight, down_weight=down_weight)


def slot_numbers(assigned):
    onehot = (assigned[..., None] == jnp.arange(EXPERTS, dtype=jnp.int32)).astype(jnp.int32)
    earlier = jnp.cumsum(onehot, axis=-2) - onehot
    return jnp.sum(earlier * onehot, axis=-1).astype(jnp.int32)


def run_expert(operands):
    row_block, gate_up, down_rows = operands
    total = jnp.dot(row_block, gate_up.reshape(D, 2 * FF), preferred_element_type=jnp.float32)
    gate_part = total[:, :FF]
    up_part = total[:, FF:]
    hidden = (jax.nn.silu(gate_part) * up_part).astype(jnp.bfloat16)
    hidden = lax.optimization_barrier(hidden)
    group_width = FF // N_EXPERT
    grouped = hidden.reshape(-1, N_EXPERT, group_width).astype(jnp.float32)
    down_grouped = down_rows.reshape(N_EXPERT, group_width, D).astype(jnp.float32)
    partial_sum = jnp.einsum("rjf,jfd->jrd", grouped, down_grouped).astype(jnp.bfloat16)
    partial_sum = lax.optimization_barrier(partial_sum)
    return jnp.sum(partial_sum.astype(jnp.float32), axis=0).astype(jnp.bfloat16)


def reference(tokens, routes, gate_weights, gate_up_weight, down_weight):
    shards = routes.reshape(N_DP, TOK_DEV * TOPK).astype(jnp.int32)
    slot_index = slot_numbers(shards)
    source = jnp.broadcast_to(jnp.arange(N_DP, dtype=jnp.int32)[:, None], shards.shape)
    dest_index = ((shards * N_DP + source) * CAP + slot_index).reshape(-1).astype(jnp.int32)
    token_ids = jnp.repeat(jnp.arange(TOKENS, dtype=jnp.int32), TOPK)
    holder = jnp.full((EXPERTS * N_DP * CAP,), TOKENS, dtype=jnp.int32).at[dest_index].set(token_ids)
    padded = jnp.concatenate([tokens, jnp.zeros((1, D), tokens.dtype)], axis=0)
    dispatched = padded[holder].reshape(EXPERTS, N_DP * CAP, D)
    expert_out = lax.map(run_expert, (dispatched, gate_up_weight, down_weight))
    lookup = expert_out.reshape(EXPERTS * N_DP * CAP, D)
    picked = lookup[dest_index].reshape(TOKENS, TOPK, D).astype(jnp.float32)
    return jnp.sum(gate_weights[:, :, None] * picked, axis=1).astype(jnp.bfloat16)
```

```python
from functools import partial

import jax
import jax.numpy as jnp
from jax import lax
from jax.experimental import pallas as pl
from jax.experimental.pallas import tpu as pltpu
from jax.sharding import PartitionSpec as P

CORES = 2


def slot_numbers(assigned, count):
    onehot = (assigned[:, None] == jnp.arange(count, dtype=jnp.int32)[None, :]).astype(jnp.int32)
    earlier = jnp.cumsum(onehot, axis=0) - onehot
    return jnp.sum(earlier * onehot, axis=1)


def activate(total, width_dev):
    gate_part = total[:, :width_dev]
    up_part = total[:, width_dev:]
    return (jax.nn.silu(gate_part) * up_part).astype(jnp.bfloat16)


def routed(tokens, routes, gate_weights, gate_up_weight, down_weight):
    tok_rows = tokens.shape[0]
    feature_cols = tokens.shape[1]
    groups = lax.axis_size("dp")
    capacity = 5 * tok_rows // groups
    assigned = routes.reshape(-1)
    slot_index = slot_numbers(assigned, groups)
    dest_index = assigned * capacity + slot_index
    copies = jnp.repeat(tokens, routes.shape[1], axis=0)
    outgoing = jnp.zeros((groups * capacity, feature_cols), jnp.bfloat16).at[dest_index].set(copies)
    incoming = lax.all_to_all(
        outgoing.reshape(groups, capacity, feature_cols), "dp", split_axis=0, concat_axis=0, tiled=True
    )
    width_dev = down_weight.shape[1]
    model_width = down_weight.shape[2]
    gate_up = gate_up_weight.reshape(model_width, 2 * width_dev)
    down_rows = down_weight.reshape(width_dev, model_width)
    row_block = lax.all_gather(incoming.reshape(-1, feature_cols), "expert", axis=1, tiled=True)
    total = jnp.dot(row_block, gate_up, preferred_element_type=jnp.float32)
    partial_sum = jnp.dot(activate(total, width_dev), down_rows, preferred_element_type=jnp.float32)
    partial_sum = partial_sum.reshape(groups, capacity, model_width)
    summed = lax.psum_scatter(
        partial_sum.astype(jnp.bfloat16), "expert", scatter_dimension=2, tiled=True
    )
    returned = lax.all_to_all(summed, "dp", split_axis=0, concat_axis=0, tiled=True)
    lookup = returned.reshape(groups * capacity, feature_cols)
    picked = lookup[dest_index].reshape(tok_rows, routes.shape[1], feature_cols).astype(jnp.float32)
    return jnp.sum(gate_weights[:, :, None] * picked, axis=1).astype(jnp.bfloat16)


def expert_kernel(
    rows, cols, idx_ref, oa_ref, ob_ref, pa_ref, pb_ref, wo_ref, wp_ref, gu_ref, dn_ref,
    keep_ref, send_ref, other_ref, x_ref,
):
    expert = idx_ref[8]
    lane = lax.broadcasted_iota(jnp.int32, wo_ref.shape, 1)
    for side, (a_ref, b_ref, w_ref) in enumerate(((oa_ref, ob_ref, wo_ref), (pa_ref, pb_ref, wp_ref))):
        starts = [pl.multiple_of(idx_ref[4 * side + q] * cols, cols) for q in range(4)]
        for q in range(4):
            part = (a_ref if q < 2 else b_ref)[(q % 2) * rows:(q % 2 + 1) * rows, :]
            x_ref[:, pl.ds(starts[q], cols)] = part
        x = x_ref[...]
        scale = jnp.sum(jnp.where(lane == expert, w_ref[...], 0.0), axis=1, keepdims=True)
        dims = (((1,), (1,)), ((), ()))
        gate = lax.dot_general(x, gu_ref[0], dims, preferred_element_type=jnp.float32)
        up = lax.dot_general(x, gu_ref[1], dims, preferred_element_type=jnp.float32)
        hidden = (gate / (1.0 + jnp.exp(-gate)) * up * scale).astype(jnp.bfloat16)
        for q in range(4):
            y = jnp.dot(hidden, dn_ref[:, pl.ds(starts[q], cols)], preferred_element_type=jnp.float32)
            y = y.astype(jnp.bfloat16)
            if side == 1:
                other_ref[q * rows:(q + 1) * rows, :] = y
            elif q < 2:
                keep_ref[q * rows:(q + 1) * rows, :] = y
            else:
                send_ref[(q - 2) * rows:(q - 1) * rows, :] = y


def expert_rows(index, own_a, own_b, other_a, other_b, w_own, w_other, gate_up, down):
    rows, cols = own_a.shape[0] // 2, own_a.shape[1]
    width, model = down.shape
    vmem = pl.BlockSpec(memory_space=pltpu.VMEM)
    half = jax.ShapeDtypeStruct((2 * rows, cols), jnp.bfloat16)
    return pl.pallas_call(
        partial(expert_kernel, rows, cols),
        out_shape=(half, half, jax.ShapeDtypeStruct((4 * rows, cols), jnp.bfloat16)),
        in_specs=[pl.BlockSpec(memory_space=pltpu.SMEM)] + [vmem] * 8,
        out_specs=(vmem,) * 3,
        scratch_shapes=[pltpu.VMEM((rows, model), jnp.bfloat16)],
        compiler_params=pltpu.CompilerParams(vmem_limit_bytes=40 << 20),
        cost_estimate=pl.CostEstimate(
            flops=12 * rows * width * model, bytes_accessed=6 * width * model + 32 * rows * cols, transcendentals=2 * rows * width
        ),
    )(index, own_a, own_b, other_a, other_b, w_own, w_other, gate_up, down)


def dense(groups_of, tokens, routes, gate_weights, gate_up_weight, down_weight):
    experts = lax.axis_size("dp")
    width_axis = lax.axis_size("expert")
    chips = experts // CORES
    rows, cols = tokens.shape
    width, model = down_weight.shape[1], down_weight.shape[2]
    both = ("dp", "expert")
    me, part = lax.axis_index("dp"), lax.axis_index("expert")
    core = lax.rem(me, CORES)

    def along(step):
        return [(d, d ^ (CORES * step)) for d in range(experts)]

    def plane(first):
        return [
            (d * width_axis + e, d * width_axis + (e ^ (1 if (d % CORES == 0) == first else 2)))
            for d in range(experts) for e in range(width_axis)
        ]

    swap = [(d, d ^ 1) for d in range(experts)]
    near, far = plane(True), plane(False)

    order = [jnp.stack([part, part ^ 1, part ^ 2, part ^ 3]), jnp.stack([part, part ^ 2, part ^ 1, part ^ 3])]
    own_order = jnp.where(core == 0, order[0], order[1])
    other_order = jnp.where(core == 0, order[1], order[0])
    index = jnp.concatenate([own_order, other_order, me[None]]).astype(jnp.int32)

    named = routes[:, :, None] == jnp.arange(experts, dtype=jnp.int32)[None, None, :]
    weight = jnp.sum(jnp.where(named, gate_weights[:, :, None], 0.0), axis=1)
    weight = jnp.concatenate([weight, lax.ppermute(weight, "dp", swap)], axis=1)

    gate_up = jnp.transpose(gate_up_weight.reshape(model, 2, width), (1, 2, 0))
    down = down_weight.reshape(width, model)

    held = {0: tokens}
    weights = {0: weight}
    for k in range(1, chips):
        held[k] = lax.ppermute(tokens, "dp", along(k))
        weights[k] = lax.ppermute(weight, "dp", along(k))

    def join(parts):
        return parts[0] if len(parts) == 1 else jnp.concatenate(parts, axis=0)

    total = None
    for group in groups_of(chips):
        n = rows * len(group)
        own = join([held[k] for k in group])
        w = join([weights[k] for k in group])
        pair = jnp.concatenate([own, lax.ppermute(own, both, near)], axis=0)
        rest = lax.ppermute(pair, both, far)
        other_pair = lax.ppermute(pair, "dp", swap)
        other_rest = lax.ppermute(rest, "dp", swap)
        keep, send, other = expert_rows(
            index, pair, rest, other_pair, other_rest, w[:, :experts], w[:, experts:], gate_up, down
        )
        back = lax.ppermute(other, "dp", swap)
        send = (send.astype(jnp.float32) + back[2 * n:].astype(jnp.float32)).astype(jnp.bfloat16)
        got = lax.ppermute(send, both, far)
        keep = keep.astype(jnp.float32) + back[:2 * n].astype(jnp.float32) + got.astype(jnp.float32)
        got = lax.ppermute(keep[n:].astype(jnp.bfloat16), both, near)
        keep = keep[:n] + got.astype(jnp.float32)
        for place, k in enumerate(group):
            mine = keep[place * rows:(place + 1) * rows]
            if k:
                mine = lax.ppermute(mine.astype(jnp.bfloat16), "dp", along(k)).astype(jnp.float32)
            total = mine if total is None else total + mine
    return total.astype(jnp.bfloat16)


def groups_of(chips):
    return [list(range(chips // 2)), list(range(chips // 2, chips))]


def per_device(tokens, routes, gate_weights, gate_up_weight, down_weight):
    experts, width_axis = lax.axis_size("dp"), lax.axis_size("expert")
    chips = experts // CORES
    capacity = 5 * tokens.shape[0] // experts
    square = width_axis == 4 and chips > 1 and chips & (chips - 1) == 0
    if square and tokens.shape[0] <= CORES * capacity:
        return dense(groups_of, tokens, routes, gate_weights, gate_up_weight, down_weight)
    return routed(tokens, routes, gate_weights, gate_up_weight, down_weight)


def solution(mesh):
    return jax.shard_map(
        per_device,
        mesh=mesh,
        in_specs=(
            P("dp", "expert"),
            P("dp", None),
            P("dp", None),
            P("dp", None, None, "expert"),
            P("dp", "expert", None),
        ),
        out_specs=P("dp", "expert"),
        check_vma=False,
    )
```

```python
from functools import partial

import jax
import jax.numpy as jnp
from jax import lax
from jax.experimental import pallas as pl
from jax.experimental.pallas import tpu as pltpu
from jax.sharding import PartitionSpec as P


CORES = 2
EXPERT_MIB = 14


def slot_numbers(assigned, count):
    onehot = (assigned[:, None] == jnp.arange(count, dtype=jnp.int32)[None, :]).astype(jnp.int32)
    earlier = jnp.cumsum(onehot, axis=0) - onehot
    return jnp.sum(earlier * onehot, axis=1)


def activate(total, width_dev):
    gate_part = total[:, :width_dev]
    up_part = total[:, width_dev:]
    return (jax.nn.silu(gate_part) * up_part).astype(jnp.bfloat16)


def routed(tokens, routes, gate_weights, gate_up_weight, down_weight):
    tok_rows = tokens.shape[0]
    feature_cols = tokens.shape[1]
    groups = lax.axis_size("dp")
    capacity = 5 * tok_rows // groups
    assigned = routes.reshape(-1)
    slot_index = slot_numbers(assigned, groups)
    dest_index = assigned * capacity + slot_index
    copies = jnp.repeat(tokens, routes.shape[1], axis=0)
    outgoing = jnp.zeros((groups * capacity, feature_cols), jnp.bfloat16).at[dest_index].set(copies)
    incoming = lax.all_to_all(
        outgoing.reshape(groups, capacity, feature_cols), "dp", split_axis=0, concat_axis=0, tiled=True
    )
    width_dev = down_weight.shape[1]
    model_width = down_weight.shape[2]
    gate_up = gate_up_weight.reshape(model_width, 2 * width_dev)
    down_rows = down_weight.reshape(width_dev, model_width)
    row_block = lax.all_gather(incoming.reshape(-1, feature_cols), "expert", axis=1, tiled=True)
    total = jnp.dot(row_block, gate_up, preferred_element_type=jnp.float32)
    partial_sum = jnp.dot(activate(total, width_dev), down_rows, preferred_element_type=jnp.float32)
    partial_sum = partial_sum.reshape(groups, capacity, model_width)
    summed = lax.psum_scatter(
        partial_sum.astype(jnp.bfloat16), "expert", scatter_dimension=2, tiled=True
    )
    returned = lax.all_to_all(summed, "dp", split_axis=0, concat_axis=0, tiled=True)
    lookup = returned.reshape(groups * capacity, feature_cols)
    picked = lookup[dest_index].reshape(tok_rows, routes.shape[1], feature_cols).astype(jnp.float32)
    return jnp.sum(gate_weights[:, :, None] * picked, axis=1).astype(jnp.bfloat16)


def settle_kernel(idx_ref, gate_up_w, down_w, out_ref):
    for i in range(idx_ref.shape[0]):
        out_ref[i] = idx_ref[i]


def settle(index, gate_up, down):
    smem = pl.BlockSpec(memory_space=pltpu.SMEM)
    vmem = pl.BlockSpec(memory_space=pltpu.VMEM)
    return pl.pallas_call(
        settle_kernel,
        out_shape=jax.ShapeDtypeStruct(index.shape, index.dtype),
        in_specs=[smem, vmem, vmem],
        out_specs=smem,
        compiler_params=pltpu.CompilerParams(vmem_limit_bytes=EXPERT_MIB << 20),
        name="settle",
    )(index, gate_up, down)


def expert_kernel(rows, cols, idx_ref, a_ref, b_ref, w_ref, gate_up_w, down_w, first_ref, second_ref, x_ref):
    starts = [pl.multiple_of(idx_ref[q] * cols, cols) for q in range(4)]
    for q in range(4):
        part = (a_ref if q < 2 else b_ref)[(q % 2) * rows:(q % 2 + 1) * rows, :]
        x_ref[:, pl.ds(starts[q], cols)] = part
    x = x_ref[...]
    line = lax.broadcasted_iota(jnp.int32, w_ref.shape, 0)
    scale = jnp.sum(jnp.where(line == idx_ref[4], w_ref[...], 0.0), axis=0, keepdims=True).T
    dims = (((1,), (1,)), ((), ()))
    gate = lax.dot_general(x, gate_up_w[0], dims, preferred_element_type=jnp.float32)
    up = lax.dot_general(x, gate_up_w[1], dims, preferred_element_type=jnp.float32)
    hidden = (gate / (1.0 + jnp.exp(-gate)) * up * scale).astype(jnp.bfloat16)
    for q in (2, 3, 0, 1):
        y = jnp.dot(hidden, down_w[:, pl.ds(starts[q], cols)], preferred_element_type=jnp.float32)
        (first_ref if q < 2 else second_ref)[(q % 2) * rows:(q % 2 + 1) * rows, :] = y.astype(jnp.bfloat16)


def expert_rows(index, part_a, part_b, weight, kept):
    rows, cols = part_a.shape[0] // 2, part_a.shape[1]
    width, model = kept[1].shape
    vmem = pl.BlockSpec(memory_space=pltpu.VMEM)
    half = jax.ShapeDtypeStruct((2 * rows, cols), jnp.bfloat16)
    return pl.pallas_call(
        partial(expert_kernel, rows, cols),
        out_shape=(half, half),
        in_specs=[pl.BlockSpec(memory_space=pltpu.SMEM)] + [vmem] * 5,
        out_specs=(vmem,) * 2,
        scratch_shapes=[pltpu.VMEM((rows, model), jnp.bfloat16)],
        compiler_params=pltpu.CompilerParams(vmem_limit_bytes=EXPERT_MIB << 20),
        cost_estimate=pl.CostEstimate(
            flops=6 * rows * width * model, bytes_accessed=6 * width * model + 16 * rows * cols, transcendentals=rows * width
        ),
        name="expert",
    )(index, part_a, part_b, weight, *kept)


def dense(groups_of, tokens, routes, gate_weights, gate_up_weight, down_weight):
    experts = lax.axis_size("dp")
    width_axis = lax.axis_size("expert")
    chips = experts // CORES
    rows, _ = tokens.shape
    width, model = down_weight.shape[1], down_weight.shape[2]
    both = ("dp", "expert")
    me, part = lax.axis_index("dp"), lax.axis_index("expert")
    core = lax.rem(me, CORES)

    def along(step):
        return [(d, d ^ (CORES * step)) for d in range(experts)]

    def plane(first):
        return [
            (d * width_axis + e, d * width_axis + (e ^ (1 if (d % CORES == 0) == first else 2)))
            for d in range(experts) for e in range(width_axis)
        ]

    swap = [(d, d ^ 1) for d in range(experts)]
    near, far = plane(True), plane(False)

    order = [jnp.stack([part, part ^ 1, part ^ 2, part ^ 3]), jnp.stack([part, part ^ 2, part ^ 1, part ^ 3])]
    own_order = jnp.where(core == 0, order[0], order[1])
    other_order = jnp.where(core == 0, order[1], order[0])
    own_index = jnp.concatenate([own_order, me[None]]).astype(jnp.int32)
    other_index = jnp.concatenate([other_order, me[None]]).astype(jnp.int32)

    named = routes.T[:, None, :] == jnp.arange(experts, dtype=jnp.int32)[None, :, None]
    weight = jnp.sum(jnp.where(named, gate_weights.T[:, None, :], 0.0), axis=0)

    gate_up = jnp.transpose(gate_up_weight.reshape(model, 2, width), (1, 2, 0))
    down = down_weight.reshape(width, model)
    kept = gate_up, down
    index = settle(jnp.concatenate([own_index, other_index]), *kept)
    own_index, other_index = index[:5], index[5:]

    def join(parts):
        return parts[0] if len(parts) == 1 else jnp.concatenate(parts, axis=0)

    held = {0: tokens}
    weights = {0: weight}
    for k in range(1, chips):
        held[k] = lax.ppermute(tokens, "dp", along(k))
    for k in range(1, chips):
        weights[k] = lax.ppermute(weight, "dp", along(k))
    plan = groups_of(chips)
    own_weight = jnp.concatenate([weights[k] for group in plan for k in group], axis=1)
    other_weight = lax.ppermute(own_weight, "dp", swap)

    total, top = None, 0
    for group in plan:
        n = rows * len(group)
        own = join([held[k] for k in group])
        pair = jnp.concatenate([own, lax.ppermute(own, both, near)], axis=0)
        rest = lax.ppermute(pair, both, far)
        other_pair = lax.ppermute(pair, "dp", swap)
        other_rest = lax.ppermute(rest, "dp", swap)
        parts = expert_rows(other_index, other_pair, other_rest, other_weight[:, top:top + n], kept)
        back = [lax.ppermute(parts[i], "dp", swap).astype(jnp.float32) for i in (1, 0)]
        keep, give = expert_rows(own_index, pair, rest, own_weight[:, top:top + n], kept)
        got = lax.ppermute((give.astype(jnp.float32) + back[0]).astype(jnp.bfloat16), both, far)
        keep = keep.astype(jnp.float32) + back[1] + got.astype(jnp.float32)
        got = lax.ppermute(keep[n:].astype(jnp.bfloat16), both, near)
        keep = keep[:n] + got.astype(jnp.float32)
        top += n
        for at, k in enumerate(group):
            mine = keep[at * rows:(at + 1) * rows]
            if k:
                mine = lax.ppermute(mine.astype(jnp.bfloat16), "dp", along(k)).astype(jnp.float32)
            total = mine if total is None else total + mine
    return total.astype(jnp.bfloat16)


def groups_of(chips):
    return [[0, *range(chips // 2 + 1, chips)], list(range(1, chips // 2 + 1))]


def per_device(tokens, routes, gate_weights, gate_up_weight, down_weight):
    experts, width_axis = lax.axis_size("dp"), lax.axis_size("expert")
    chips = experts // CORES
    capacity = 5 * tokens.shape[0] // experts
    square = width_axis == 4 and chips > 1 and chips & (chips - 1) == 0
    if square and tokens.shape[0] <= CORES * capacity:
        return dense(groups_of, tokens, routes, gate_weights, gate_up_weight, down_weight)
    return routed(tokens, routes, gate_weights, gate_up_weight, down_weight)


def solution(mesh):
    return jax.shard_map(
        per_device,
        mesh=mesh,
        in_specs=(
            P("dp", "expert"),
            P("dp", None),
            P("dp", None),
            P("dp", None, None, "expert"),
            P("dp", "expert", None),
        ),
        out_specs=P("dp", "expert"),
        check_vma=False,
    )
```

```python
from functools import partial

import jax
import jax.numpy as jnp
from jax import lax
from jax.experimental import pallas as pl
from jax.experimental.pallas import tpu as pltpu
from jax.sharding import PartitionSpec as P


CORES = 2
EXPERT_MIB = 14


def slot_numbers(assigned, count):
    onehot = (assigned[:, None] == jnp.arange(count, dtype=jnp.int32)[None, :]).astype(jnp.int32)
    earlier = jnp.cumsum(onehot, axis=0) - onehot
    return jnp.sum(earlier * onehot, axis=1)


def activate(total, width_dev):
    gate_part = total[:, :width_dev]
    up_part = total[:, width_dev:]
    return (jax.nn.silu(gate_part) * up_part).astype(jnp.bfloat16)


def routed(tokens, routes, gate_weights, gate_up_weight, down_weight):
    tok_rows = tokens.shape[0]
    feature_cols = tokens.shape[1]
    groups = lax.axis_size("dp")
    capacity = 5 * tok_rows // groups
    assigned = routes.reshape(-1)
    slot_index = slot_numbers(assigned, groups)
    dest_index = assigned * capacity + slot_index
    copies = jnp.repeat(tokens, routes.shape[1], axis=0)
    outgoing = jnp.zeros((groups * capacity, feature_cols), jnp.bfloat16).at[dest_index].set(copies)
    incoming = lax.all_to_all(
        outgoing.reshape(groups, capacity, feature_cols), "dp", split_axis=0, concat_axis=0, tiled=True
    )
    width_dev = down_weight.shape[1]
    model_width = down_weight.shape[2]
    gate_up = gate_up_weight.reshape(model_width, 2 * width_dev)
    down_rows = down_weight.reshape(width_dev, model_width)
    row_block = lax.all_gather(incoming.reshape(-1, feature_cols), "expert", axis=1, tiled=True)
    total = jnp.dot(row_block, gate_up, preferred_element_type=jnp.float32)
    partial_sum = jnp.dot(activate(total, width_dev), down_rows, preferred_element_type=jnp.float32)
    partial_sum = partial_sum.reshape(groups, capacity, model_width)
    summed = lax.psum_scatter(
        partial_sum.astype(jnp.bfloat16), "expert", scatter_dimension=2, tiled=True
    )
    returned = lax.all_to_all(summed, "dp", split_axis=0, concat_axis=0, tiled=True)
    lookup = returned.reshape(groups * capacity, feature_cols)
    picked = lookup[dest_index].reshape(tok_rows, routes.shape[1], feature_cols).astype(jnp.float32)
    return jnp.sum(gate_weights[:, :, None] * picked, axis=1).astype(jnp.bfloat16)


def settle_kernel(w_ref, out_ref):
    out_ref[...] = jnp.zeros_like(out_ref)


def settle(weight):
    vmem = pl.BlockSpec(memory_space=pltpu.VMEM)
    return pl.pallas_call(
        settle_kernel,
        out_shape=jax.ShapeDtypeStruct((8, 128), jnp.float32),
        in_specs=[vmem],
        out_specs=vmem,
        compiler_params=pltpu.CompilerParams(vmem_limit_bytes=EXPERT_MIB << 20, has_side_effects=True),
        name="settle",
    )(weight)


def expert_kernel(side, rows, cols, idx_ref, a_ref, b_ref, w_ref, gate_up_w, down_w, *refs):
    outs, x_ref = refs[:-1], refs[-1]
    starts = [pl.multiple_of(idx_ref[4 * side + q] * cols, cols) for q in range(4)]
    for q in range(4):
        x_ref[:, pl.ds(starts[q], cols)] = (a_ref if q < 2 else b_ref)[(q % 2) * rows:(q % 2 + 1) * rows, :]
    x = x_ref[...]
    line = lax.broadcasted_iota(jnp.int32, w_ref.shape, 0)
    scale = jnp.sum(jnp.where(line == idx_ref[8], w_ref[...], 0.0), axis=0, keepdims=True).T
    dims = (((1,), (1,)), ((), ()))
    gate = lax.dot_general(x, gate_up_w[0], dims, preferred_element_type=jnp.float32)
    up = lax.dot_general(x, gate_up_w[1], dims, preferred_element_type=jnp.float32)
    hidden = (gate / (1.0 + jnp.exp(-gate)) * up * scale).astype(jnp.bfloat16)
    held = 4 // len(outs)
    for q in (2, 3, 0, 1):
        y = jnp.dot(hidden, down_w[:, pl.ds(starts[q], cols)], preferred_element_type=jnp.float32)
        outs[q // held][(q % held) * rows:(q % held + 1) * rows, :] = y.astype(jnp.bfloat16)


def expert_rows(side, index, pair, rest, weight, kept):
    rows, cols = pair.shape[0] // 2, pair.shape[1]
    width, model = kept[1].shape
    vmem = pl.BlockSpec(memory_space=pltpu.VMEM)
    outs = 1 if side else 2
    return pl.pallas_call(
        partial(expert_kernel, side, rows, cols),
        out_shape=(jax.ShapeDtypeStruct((4 // outs * rows, cols), jnp.bfloat16),) * outs,
        in_specs=[pl.BlockSpec(memory_space=pltpu.SMEM)] + [vmem] * 5,
        out_specs=(vmem,) * outs,
        scratch_shapes=[pltpu.VMEM((rows, model), jnp.bfloat16)],
        compiler_params=pltpu.CompilerParams(vmem_limit_bytes=EXPERT_MIB << 20),
        cost_estimate=pl.CostEstimate(
            flops=6 * rows * width * model, bytes_accessed=6 * width * model + 16 * rows * cols, transcendentals=rows * width
        ),
        name="expert",
    )(index, pair, rest, weight, *kept)


def dense(tokens, routes, gate_weights, gate_up_weight, down_weight):
    experts = lax.axis_size("dp")
    width_axis = lax.axis_size("expert")
    rows, _ = tokens.shape
    width, model = down_weight.shape[1], down_weight.shape[2]
    both = ("dp", "expert")
    me, part = lax.axis_index("dp"), lax.axis_index("expert")

    def along(step):
        return [(d, d ^ (CORES * step)) for d in range(experts)]

    def plane(first):
        return [
            (d * width_axis + e, d * width_axis + (e ^ (1 if (d % CORES == 0) == first else 2)))
            for d in range(experts) for e in range(width_axis)
        ]

    swap = [(d, d ^ 1) for d in range(experts)]
    near, far = plane(True), plane(False)

    core = lax.rem(me, CORES)
    steps = jnp.where(core == 0, jnp.array([0, 1, 2, 3, 0, 2, 1, 3]), jnp.array([0, 2, 1, 3, 0, 1, 2, 3]))
    index = jnp.concatenate([part ^ steps, me[None]]).astype(jnp.int32)

    gate_up = jnp.transpose(gate_up_weight.reshape(model, 2, width), (1, 2, 0))
    down = down_weight.reshape(width, model)
    kept = gate_up, down
    for weight in kept:
        settle(weight)

    def join(parts, axis=0):
        return parts[0] if len(parts) == 1 else jnp.concatenate(parts, axis=axis)

    named = routes.T[:, None, :] == jnp.arange(experts, dtype=jnp.int32)[None, :, None]
    weight = jnp.sum(jnp.where(named, gate_weights.T[:, None, :], 0.0), axis=0)
    held, weights = {0: tokens}, {0: weight}
    for k, source, step in ((2, 0, 2), (1, 0, 1), (3, 2, 1)):
        held[k] = lax.ppermute(held[source], "dp", along(step))
        weights[k] = lax.ppermute(weights[source], "dp", along(step))
    plan = [[1, 2]], [[0], [3]]
    shards = [k for group in plan for batch in group for k in batch]
    own_weight = join([weights[k] for k in shards], axis=1)
    other_weight = lax.ppermute(own_weight, "dp", swap)

    sums, top = {}, 0
    for group in plan:
        members = [k for batch in group for k in batch]
        n = rows * len(members)
        own = [join([held[k] for k in batch]) for batch in group]
        met = [lax.ppermute(part, both, near) for part in own]
        pair = join(own + met)
        rest = lax.ppermute(pair, both, far)
        other_pair = lax.ppermute(pair, "dp", swap)
        other_rest = lax.ppermute(rest, "dp", swap)
        span = slice(top, top + n)
        keep, give = expert_rows(0, index, pair, rest, own_weight[:, span], kept)
        other, = expert_rows(1, index, other_pair, other_rest, other_weight[:, span], kept)
        back = lax.ppermute(other, "dp", swap)
        give = give.astype(jnp.float32) + back[2 * n:].astype(jnp.float32)
        got = lax.ppermute(give.astype(jnp.bfloat16), both, far)
        keep = keep.astype(jnp.float32) + back[:2 * n].astype(jnp.float32) + got.astype(jnp.float32)
        got = lax.ppermute(keep[n:].astype(jnp.bfloat16), both, near)
        keep = keep[:n] + got.astype(jnp.float32)
        top += n
        for at, k in enumerate(members):
            sums[k] = keep[at * rows:(at + 1) * rows]
    passed = lax.ppermute(sums[2].astype(jnp.bfloat16), "dp", along(1))
    passed = (sums[3] + passed.astype(jnp.float32)).astype(jnp.bfloat16)
    total = sums[0] + lax.ppermute(sums[1].astype(jnp.bfloat16), "dp", along(1)).astype(jnp.float32)
    total = total + lax.ppermute(passed, "dp", along(3)).astype(jnp.float32)
    return total.astype(jnp.bfloat16)


def per_device(tokens, routes, gate_weights, gate_up_weight, down_weight):
    experts, width_axis = lax.axis_size("dp"), lax.axis_size("expert")
    chips = experts // CORES
    capacity = 5 * tokens.shape[0] // experts
    square = width_axis == 4 and chips == 4
    if square and tokens.shape[0] <= CORES * capacity:
        return dense(tokens, routes, gate_weights, gate_up_weight, down_weight)
    return routed(tokens, routes, gate_weights, gate_up_weight, down_weight)


def solution(mesh):
    return jax.shard_map(
        per_device,
        mesh=mesh,
        in_specs=(
            P("dp", "expert"),
            P("dp", None),
            P("dp", None),
            P("dp", None, None, "expert"),
            P("dp", "expert", None),
        ),
        out_specs=P("dp", "expert"),
        check_vma=False,
    )
```
